512 devices in a mesh: dp: 8 (over z), expert: 64 (over x, y, core).
Axes of the slice: x: 4, y: 8, z: 8, core: 2. Of those that a mesh axis runs over, the one named last changes fastest.
Arguments:
- tokens: bfloat16 [1024, 2048], P(('dp', 'expert')), may hold values from -6 to 6
- combine: bfloat16 [1024], P(('dp', 'expert')), may hold values from 0.099609375 to 1
- routes: int32 [1024], P(('dp', 'expert')), may hold values from 0 to 7, as said below
- capacity_slot: int32 [1024], P(('dp', 'expert')), may hold values from -1 to 19, as said below
- readout: float32 [2048], replicated, may hold values from -6 to 6
- weight_in: bfloat16 [8, 2048, 14336], P('dp', None, 'expert'), may hold values from -0.125 to 0.125
- weight_out: bfloat16 [8, 14336, 2048], P('dp', 'expert'), may hold values from -0.046875 to 0.046875
Outputs:
- r2_grad: bfloat16 [1024, 2048], P(('dp', 'expert'))
- grad_in: bfloat16 [8, 2048, 14336], P('dp', None, 'expert')
- grad_out: bfloat16 [8, 14336, 2048], P('dp', 'expert')
The draws below stay inside these ranges and needn't reach their ends.
Inputs may be any that keep to these rules, and one draw needn't show every extreme that they name: `routes`: each token's expert. `capacity_slot`: in each aligned block of 128 tokens, the tokens routed to one expert carry slots 0, 1, 2, ... in token order while fewer than 20 came before them, and -1 after; in every block some expert receives 30 tokens or more, so its 20 slots are full.
All inputs are finite; a program needn't handle non-finite values.
Results may differ from the reference program's by a relative error of at most 0.006.
Values may be sent and summed in bfloat16 or wider, within the bound.
A program may use at most 64 MiB of HBM per device.

```python
import jax
import jax.numpy as jnp
from jax import lax

D = 2048
FF = 14336
GROUP_TOK = 128
TOKENS = 1024
EXPERTS = 8
CAP = 20
HOT = 30
N_DP = 8


def route_plan(key):
    group_keys = jax.random.split(jax.random.fold_in(key, 7), N_DP)

    def one_group(group_key):
        hot_key, other_key, order_key = jax.random.split(group_key, 3)
        hot_expert = jax.random.randint(hot_key, (), 0, EXPERTS)
        others = jax.random.randint(other_key, (GROUP_TOK,), 0, EXPERTS)
        order_perm = jax.random.permutation(order_key, GROUP_TOK)
        marked = jnp.zeros((GROUP_TOK,), jnp.int32).at[order_perm[:HOT]].set(1)
        chosen = jnp.where(marked == 1, hot_expert, others).astype(jnp.int32)
        onehot = (chosen[:, None] == jnp.arange(EXPERTS, dtype=jnp.int32)[None, :]).astype(jnp.int32)
        before = jnp.cumsum(onehot, axis=0) - onehot
        rank_seen = jnp.sum(before * onehot, axis=1)
        slot_value = jnp.where(rank_seen < CAP, rank_seen, -1).astype(jnp.int32)
        return (chosen, slot_value)
    chosen, slot_value = jax.vmap(one_group)(group_keys)
    return (chosen.reshape(-1), slot_value.reshape(-1))


def draw_routes(key, part):
    return route_plan(key)[0]


def draw_capacity_slot(key, part):
    return route_plan(key)[1]


def block_scale(key, dims, pieces, smallest, top_value):
    factor_of = 1.0
    for axis_at, shards_of in pieces:
        steps = jax.random.uniform(jax.random.fold_in(jax.random.fold_in(key, 6), axis_at), (shards_of,), jnp.float32, smallest / len(pieces), top_value / len(pieces))
        factor_of = factor_of * jnp.repeat(jnp.exp(steps), dims[axis_at] // shards_of).reshape((-1,) + (1,) * (len(dims) - 1 - axis_at))
    return factor_of


def centred(own_key, shape, spread, most, shards=(), kind=jnp.bfloat16):
    drawn = jax.random.normal(own_key, shape, jnp.float32) * spread
    if len(shards) > 0:
        drawn = block_scale(own_key, shape, shards, -0.22, 0.18) * drawn
    return jnp.clip(drawn, min=-most, max=most).astype(kind)


def setup_inputs(seed: int = 0) -> dict:
    seeds = jax.random.split(jax.random.key(seed), 8)
    return {
        "tokens": centred(seeds[0], (TOKENS, D), 1.0, 6.0, ((0, 512),)),
        "combine": jnp.clip(0.099609375 + 0.9003906 * jax.random.uniform(seeds[1], (TOKENS,), jnp.float32) ** block_scale(seeds[1], (TOKENS,), ((0, 512),), -0.2, 0.2), 0.099609375, 1.0).astype(jnp.bfloat16),
        "routes": draw_routes(jax.random.fold_in(seeds[7], 71), 0),
        "capacity_slot": draw_capacity_slot(jax.random.fold_in(seeds[7], 71), 0),
        "readout": centred(seeds[4], (D,), 1.0, 6.0, (), jnp.float32),
        "weight_in": centred(seeds[5], (EXPERTS, D, FF), D ** -0.5, 0.125, ((0, 8), (2, 64))),
        "weight_out": centred(seeds[6], (EXPERTS, FF, D), FF ** -0.5, 0.046875, ((0, 8), (1, 64))),
    }


def expert_pass(rows_in, rows_c, readout, matrix_in, matrix_out):
    combine_col = rows_c.astype(jnp.float32)[:, None]
    head_row = readout[None, :]
    pre_act = jnp.dot(rows_in, matrix_in, preferred_element_type=jnp.float32)
    sigm = jax.nn.sigmoid(pre_act)
    slope_act = sigm * (1.0 + pre_act * (1.0 - sigm))
    bend_act = sigm * (1.0 - sigm) * (2.0 + pre_act * (1.0 - 2.0 * sigm))
    hidden = (pre_act * sigm).astype(jnp.bfloat16)
    mixed_sum = combine_col * jnp.dot(hidden, matrix_out, preferred_element_type=jnp.float32)
    tangent = jnp.tanh(rows_in.astype(jnp.float32) + mixed_sum)
    sech_sq = 1.0 - tangent * tangent
    upstream = head_row * sech_sq
    upstream_rows = upstream.astype(jnp.bfloat16)
    back_hidden = combine_col * jnp.dot(upstream_rows, matrix_out.T, preferred_element_type=jnp.float32)
    back_pre = (back_hidden * slope_act).astype(jnp.bfloat16)
    grad_rows = (upstream + jnp.dot(back_pre, matrix_in.T, preferred_element_type=jnp.float32)).astype(jnp.bfloat16)
    second = jnp.dot(grad_rows, matrix_in, preferred_element_type=jnp.float32)
    push_rows = (combine_col * second * slope_act).astype(jnp.bfloat16)
    total_push = grad_rows.astype(jnp.float32) + jnp.dot(push_rows, matrix_out, preferred_element_type=jnp.float32)
    curve_term = total_push * head_row * (-2.0 * tangent * sech_sq)
    echo_rows = (combine_col * curve_term).astype(jnp.bfloat16)
    back_second = jnp.dot(echo_rows, matrix_out.T, preferred_element_type=jnp.float32)
    final_pre = (back_second * slope_act + second * back_hidden * bend_act).astype(jnp.bfloat16)
    grad_in = (jnp.dot(grad_rows.T, back_pre, preferred_element_type=jnp.float32)
               + jnp.dot(rows_in.T, final_pre, preferred_element_type=jnp.float32)).astype(jnp.bfloat16)
    grad_out = (jnp.dot(push_rows.T, upstream_rows, preferred_element_type=jnp.float32)
                + jnp.dot(hidden.T, echo_rows, preferred_element_type=jnp.float32)).astype(jnp.bfloat16)
    return grad_rows, grad_in, grad_out


def reference(tokens, combine, routes, capacity_slot, readout, weight_in, weight_out):
    slot_total = EXPERTS * CAP
    grouped = tokens.reshape(N_DP, GROUP_TOK, D).astype(jnp.float32)
    grouped_c = combine.reshape(N_DP, GROUP_TOK).astype(jnp.float32)
    slot_place = (routes * CAP + capacity_slot).astype(jnp.int32).reshape(N_DP, GROUP_TOK)
    kept = (capacity_slot >= 0).reshape(N_DP, GROUP_TOK)
    slot_index = jnp.arange(slot_total, dtype=jnp.int32)
    onehot = ((slot_index[None, :, None] == slot_place[:, None, :]) & kept[:, None, :]).astype(jnp.float32)
    packed = jnp.einsum("rst,rtd->rsd", onehot, grouped).astype(jnp.bfloat16)
    packed_c = jnp.einsum("rst,rt->rs", onehot, grouped_c).astype(jnp.bfloat16)
    per_expert = packed.reshape(N_DP, EXPERTS, CAP, D).transpose(1, 0, 2, 3).reshape(EXPERTS, N_DP * CAP, D)
    per_expert_c = packed_c.reshape(N_DP, EXPERTS, CAP).transpose(1, 0, 2).reshape(EXPERTS, N_DP * CAP)

    def one_expert(operands):
        return expert_pass(operands[0], operands[1], readout, operands[2], operands[3])

    grad_rows, grad_in, grad_out = lax.map(one_expert, (per_expert, per_expert_c, weight_in, weight_out))
    home_rows = grad_rows.reshape(EXPERTS, N_DP, CAP, D).transpose(1, 0, 2, 3).reshape(N_DP, slot_total, D)
    clipped = jnp.clip(slot_place, 0, slot_total - 1).astype(jnp.int32)
    picked = jax.vmap(lambda rows, where_at: jnp.take(rows, where_at, axis=0))(home_rows, clipped)
    picked = picked.reshape(TOKENS, D)
    tangent_home = jnp.tanh(tokens.astype(jnp.float32))
    dropped = (readout[None, :] * (1.0 - tangent_home * tangent_home)).astype(jnp.bfloat16)
    r2_grad = jnp.where((capacity_slot >= 0)[:, None], picked, dropped)
    return r2_grad, grad_in, grad_out
```

```python
import functools

import jax
import jax.numpy as jnp
from jax import lax
from jax.experimental import pallas as pl
from jax.experimental.pallas import tpu as pltpu
from jax.sharding import PartitionSpec as P

MESH = pl.DeviceIdType.MESH
F32 = jnp.float32
BF16 = jnp.bfloat16
BLK = 256
META = 128
SUB = 8
TAIL = 8


def dot(a, b, dims):
    return lax.dot_general(a, b, ((dims[:1], dims[1:]), ((), ())), preferred_element_type=F32)


def kernel(cfg, ext_ref, meta_ref, head_ref, w1_hbm, w2_hbm, gin_ref, gout_ref, r2_ref, *scratch):
    nz, nx, ny, cap = cfg
    (w1, w2, wsem, ssem, rsem, dr, ay, zs, zr, mr, rb, rpart, cbc, ownf, cs, cr, xs, xr, ys, yr, ab,
     fb, ts, tr) = scratch
    nb = 2 * nx
    rows = nz * cap
    tiles = rows // SUB
    nq = ny // 2
    per_q = tiles // nq
    capp = -(-cap // SUB) * SUB
    z = lax.axis_index("dp")
    j = lax.axis_index("expert")
    c = lax.rem(j, 2)
    y = lax.rem(j // 2, ny)
    x = j // (2 * ny)
    bid = 2 * x + c
    q, h = y // 2, lax.rem(y, 2)

    def at(px, py, pc):
        return {"expert": (px * ny + py) * 2 + pc}

    def ring(v, k, n):
        return lax.rem(v + k + n, n)

    partner = at(x, y, 1 - c)
    sends = []
    used = [0]

    def slots(n):
        base = used[0]
        used[0] += n
        return base

    def send(src, dst, sem, dev):
        copy = pltpu.make_async_remote_copy(
            src_ref=src, dst_ref=dst, send_sem=ssem.at[sem], recv_sem=rsem.at[sem],
            device_id=dev, device_id_type=MESH)
        copy.start()
        sends.append(copy)
        return copy

    w1_copy = pltpu.make_async_copy(w1_hbm, w1, wsem.at[0])
    w2_copy = pltpu.make_async_copy(w2_hbm, w2, wsem.at[1])
    w1_copy.start()
    w2_copy.start()

    barrier = pltpu.get_barrier_semaphore()
    peers = [partner]
    peers += [at(ring(x, k, nx), y, pc) for k in range(1, nx) for pc in range(2)]
    peers += [at(x, ring(y, k, ny), c) for k in range(1, ny)]
    peers += [{"dp": ring(z, k, nz)} for k in range(1, nz)]
    for dev in peers:
        pl.semaphore_signal(barrier, inc=1, device_id=dev, device_id_type=MESH)
    pl.semaphore_wait(barrier, len(peers))

    base = slots(nb)
    got = []
    for k in range(nx):
        for pc in range(2):
            if k == 0 and pc == 0:
                continue
            px, qc = ring(x, k, nx), lax.rem(c + pc, 2)
            got.append(send(ext_ref.at[2 * px + qc], dr.at[2 * k + pc], base + 2 * k + pc, at(px, y, qc)))
    base = slots(nz)
    got_meta = [send(meta_ref, mr.at[z], base + k, {"dp": ring(z, k, nz)}) for k in range(1, nz)]
    mr[z] = meta_ref[...]

    width = BLK + META
    n_tok = ny * 2 * nb
    lane = lax.broadcasted_iota(jnp.int32, (n_tok, nz * capp), 1)
    slot_id = jnp.full((n_tok, nz * capp), -2, jnp.int32)
    for e in range(nz):
        inside = (lane >= e * capp) & (lane < e * capp + cap)
        slot_id = jnp.where(inside, lane - e * (capp - cap), slot_id)
    slot_id = slot_id.astype(F32)
    row_i = lax.broadcasted_iota(jnp.int32, (rows, nz * capp), 0)
    col_i = lax.broadcasted_iota(jnp.int32, (rows, nz * capp), 1)
    squeeze = jnp.zeros((rows, nz * capp), F32)
    for e in range(nz):
        inside = (col_i >= e * capp) & (col_i < e * capp + cap)
        squeeze = jnp.where(inside & (row_i == col_i - e * (capp - cap)), 1.0, squeeze)
    squeeze = squeeze.astype(BF16)

    mine = ext_ref[bid].astype(F32)
    for i, copy in enumerate(got):
        copy.wait_recv()
        mine = mine + dr[i + 1].astype(F32)
    ay[y] = mine.astype(BF16)
    base = slots(ny)
    got = [send(ay.at[y], ay.at[y], base + k, at(x, ring(y, k, ny), c)) for k in range(1, ny)]
    for copy in got:
        copy.wait_recv()
    group = ay[...].reshape(n_tok, width)
    place = group[:, BLK:].astype(F32)[:, 0:1]
    onehot = jnp.where(place == slot_id, 1.0, 0.0).astype(BF16)
    packed = dot(onehot, group, (0, 0))
    zs[...] = packed.reshape(nz, capp // SUB, SUB, width).astype(BF16)

    base = slots(nz)
    got = [send(zs.at[ring(z, k, nz)], zr.at[z], base + k, {"dp": ring(z, k, nz)}) for k in range(1, nz)]
    zr[z] = zs[z]
    for copy in got:
        copy.wait_recv()
    spread = zr[...].astype(F32).reshape(nz * capp, width).astype(BF16)
    mine = dot(squeeze, spread, (1, 0))
    rb[bid] = mine[:, :BLK].astype(BF16)
    comb = mine[:, BLK + 1:BLK + 2]
    cbc[...] = jnp.broadcast_to(comb, (rows, 128)).reshape(tiles, SUB, 128)
    for i in range(2):
        rpart[i] = mine[:, 128 * i:128 * (i + 1)].reshape(tiles, SUB, 128)

    def spread_blocks(buf, use):
        base = slots(nx)
        base2 = slots(nx)
        got = [send(buf.at[bid], buf.at[bid], base + k, at(ring(x, k, nx), y, c)) for k in range(1, nx)]
        twin = [send(buf.at[bid], buf.at[bid], base2, partner)]
        use(bid)
        for k in range(1, nx):
            got[k - 1].wait_recv()
            b = 2 * ring(x, -k, nx) + c
            twin.append(send(buf.at[b], buf.at[b], base2 + k, partner))
            use(b)
        for k in range(nx):
            twin[k].wait_recv()
            use(2 * ring(x, -k, nx) + 1 - c)

    def cols(b):
        return pl.ds(pl.multiple_of(b * BLK, BLK), BLK)

    w1_copy.wait()
    w2_copy.wait()
    acc = [jnp.zeros((rows, w1.shape[1]), F32)]

    def use_rows(b):
        acc[0] = acc[0] + dot(rb[b], w1[cols(b), :], (1, 0))

    spread_blocks(rb, use_rows)
    pre = acc[0]
    sigm = jax.nn.sigmoid(pre)
    slope = sigm * (1.0 + pre * (1.0 - sigm))
    bend = sigm * (1.0 - sigm) * (2.0 + pre * (1.0 - 2.0 * sigm))
    hidden = (pre * sigm).astype(BF16)

    def tiled(v):
        return [v[:, 128 * i:128 * (i + 1)].reshape(tiles, SUB, 128) for i in range(2)]

    def flat(halves):
        return jnp.concatenate([p.reshape(rows, 128) for p in halves], axis=1)

    def loaded(ref):
        return flat([ref[i].astype(F32) for i in range(2)])

    def store(ref, v):
        for i, p in enumerate(tiled(v)):
            ref[i] = p.astype(BF16)

    def reduce_round(rd, part):
        base = slots(nx)
        base2 = slots(nx)
        base3 = slots(ny)
        got = []
        for k in range(nx):
            store(cs.at[rd, k], part(2 * ring(x, k + 1, nx) + 1 - c))
            got.append(send(cs.at[rd, k], cr.at[rd, k], base + k, partner))
        got_x = []
        for k in range(nx):
            px = ring(x, k + 1, nx)
            v = part(2 * px + c)
            got[k].wait_recv()
            v = v + loaded(cr.at[rd, k])
            if k < nx - 1:
                store(xs.at[rd, k], v)
                got_x.append(send(xs.at[rd, k], xr.at[rd, k], base2 + k, at(px, y, c)))
        for k in range(nx - 1):
            got_x[k].wait_recv()
            v = v + loaded(xr.at[rd, k])
        for i, p in enumerate(tiled(v)):
            ownf[i] = p
            ys[rd, i] = p.astype(BF16)
        got = []
        for k in range(1, ny):
            py = ring(y, k, ny)
            src = ys.at[rd, lax.rem(py, 2), pl.ds((py // 2) * per_q, per_q)]
            got.append(send(src, yr.at[rd, k], base3 + k, at(x, py, c)))
        total = ownf[h, pl.ds(q * per_q, per_q)]
        for k in range(1, ny):
            got[k - 1].wait_recv()
            total = total + yr[rd, k].astype(F32)
        return total

    def gather_round(rd, piece, use):
        ab[rd, bid, h, pl.ds(q * per_q, per_q)] = piece
        base = slots(ny)
        spot = ab.at[rd, bid, h, pl.ds(q * per_q, per_q)]
        got = [send(spot, spot, base + k, at(x, ring(y, k, ny), c)) for k in range(1, ny)]
        for copy in got:
            copy.wait_recv()

        def use_block(b):
            v = loaded(ab.at[rd, b]).astype(BF16)
            fb[rd, b] = v
            use(b, v)

        spread_blocks(ab.at[rd], use_block)

    r_piece = rpart[h, pl.ds(q * per_q, per_q)]
    c_piece = cbc[pl.ds(q * per_q, per_q)]
    head = head_ref[2 * bid + h]

    mixed = reduce_round(0, lambda b: comb * dot(hidden, w2[:, cols(b)], (1, 0)))
    tangent = jnp.tanh(r_piece + mixed)
    sech = 1.0 - tangent * tangent
    upstream = head * sech

    acc[0] = jnp.zeros_like(pre)

    def use_up(b, v):
        acc[0] = acc[0] + dot(v, w2[:, cols(b)], (1, 1))

    gather_round(0, upstream.astype(BF16), use_up)
    back_hidden = comb * acc[0]
    back_pre = (back_hidden * slope).astype(BF16)

    grad = reduce_round(1, lambda b: dot(back_pre, w1[cols(b), :], (1, 1)))
    grad = (upstream + grad).astype(BF16)
    acc[0] = jnp.zeros_like(pre)

    def use_grad(b, v):
        acc[0] = acc[0] + dot(v, w1[cols(b), :], (1, 0))

    gather_round(1, grad, use_grad)
    second = acc[0]
    push = (comb * second * slope).astype(BF16)

    base_tok = slots(nz)
    got_tok = []

    def tokens_home():
        for copy in got_meta:
            copy.wait_recv()
        place = mr[...].astype(F32).reshape(nz * TAIL, META)[:, 0:1]
        home = lax.broadcasted_iota(jnp.int32, (nz * TAIL, 1), 0) // TAIL
        local = place - (z * cap).astype(F32)
        target = jnp.where((local >= 0.0) & (local < cap), local + (home * cap).astype(F32), -1.0)
        pick = lax.broadcasted_iota(jnp.int32, (nz * TAIL, rows), 1).astype(F32)
        pick = jnp.where(pick == target, 1.0, 0.0).astype(BF16)
        for b in range(nb):
            v = dot(pick, fb[1, b], (1, 0))
            ts[:, :, b * BLK:(b + 1) * BLK] = v.reshape(nz, TAIL, BLK).astype(BF16)
        for k in range(1, nz):
            pz = ring(z, k, nz)
            got_tok.append(send(ts.at[pz], tr.at[k], base_tok + k, {"dp": pz}))

    tokens_home()
    pushed = reduce_round(2, lambda b: dot(push, w2[:, cols(b)], (1, 0)))
    curve = (grad.astype(F32) + pushed) * head * (-2.0 * tangent * sech)
    echo = (c_piece * curve).astype(BF16)
    acc[0] = jnp.zeros_like(pre)

    def use_echo(b, v):
        acc[0] = acc[0] + dot(v, w2[:, cols(b)], (1, 1))

    gather_round(2, echo, use_echo)
    final_pre = (acc[0] * slope + second * back_hidden * bend).astype(BF16)
    for b in range(nb):
        here = slice(b * BLK, (b + 1) * BLK)
        gin_ref[here, :] = (dot(fb[1, b], back_pre, (0, 0)) + dot(rb[b], final_pre, (0, 0))).astype(BF16)
        gout_ref[:, here] = (dot(push, fb[0, b], (0, 0)) + dot(hidden, fb[2, b], (0, 0))).astype(BF16)
    home = ts[z].astype(F32)
    for k in range(1, nz):
        got_tok[k - 1].wait_recv()
        home = home + tr[k].astype(F32)
    r2_ref[...] = home
    for copy in sends:
        copy.wait_send()


def shards(nx, tokens, combine, routes, capacity_slot, readout, weight_in, weight_out, cap=None):
    nz = lax.axis_size("dp")
    ne = lax.axis_size("expert")
    ny = ne // (2 * nx)
    nb = 2 * nx
    pair, d = tokens.shape
    f = weight_in.shape[2]
    if cap is None:
        cap = 5 * pair * ne // (4 * nz)
    rows = nz * cap
    tiles = rows // SUB
    capp = -(-cap // SUB) * SUB
    per_q = tiles // (ny // 2)
    width = BLK + META
    j = lax.axis_index("expert")
    spot = 2 * (j // (2 * ny)) + j % 2
    place = jnp.where(capacity_slot >= 0, routes * cap + capacity_slot, -1).astype(BF16)
    lane = lax.broadcasted_iota(jnp.int32, (pair, META), 1)
    meta = jnp.where(lane == 0, place[:, None], jnp.where(lane == 1, combine[:, None], 0)).astype(BF16)
    record = jnp.concatenate(
        [tokens.reshape(pair, nb, BLK).transpose(1, 0, 2), jnp.broadcast_to(meta[None], (nb, pair, META))], axis=2)
    row = lax.broadcasted_iota(jnp.int32, (1, nb * pair, 1), 1)
    ext = jnp.where(row // pair == spot, jnp.tile(record, (1, nb, 1)), 0).astype(BF16)
    meta8 = jnp.pad(meta, ((0, TAIL - pair), (0, 0)), constant_values=-1)
    head = readout.reshape(2 * nb, 1, 128)
    vm = pltpu.VMEM
    n_sem = nb + 3 * nz + ny + 2 * nx + 3 * (4 * nx + 2 * ny) + 8
    scratch = [
        vm((d, f), BF16), vm((f, d), BF16), pltpu.SemaphoreType.DMA((2,)),
        pltpu.SemaphoreType.DMA((n_sem,)), pltpu.SemaphoreType.DMA((n_sem,)),
        vm((nb, nb * pair, width), BF16), vm((ny, nb * pair, width), BF16),
        vm((nz, capp // SUB, SUB, width), BF16), vm((nz, capp // SUB, SUB, width), BF16),
        vm((nz, TAIL, META), BF16),
        vm((nb, rows, BLK), BF16), vm((2, tiles, SUB, 128), F32), vm((tiles, SUB, 128), F32),
        vm((2, tiles, SUB, 128), F32),
        vm((3, nx, 2, tiles, SUB, 128), BF16), vm((3, nx, 2, tiles, SUB, 128), BF16),
        vm((3, nx, 2, tiles, SUB, 128), BF16), vm((3, nx, 2, tiles, SUB, 128), BF16),
        vm((3, 2, tiles, SUB, 128), BF16), vm((3, ny, per_q, SUB, 128), BF16),
        vm((3, nb, 2, tiles, SUB, 128), BF16), vm((3, nb, rows, BLK), BF16),
        vm((nz, TAIL, d), BF16), vm((nz, TAIL, d), BF16),
    ]
    whole = pl.BlockSpec(memory_space=pltpu.VMEM)
    away = pl.BlockSpec(memory_space=pl.ANY)
    grad_in, grad_out, home = pl.pallas_call(
        functools.partial(kernel, (nz, nx, ny, cap)),
        out_shape=(
            jax.ShapeDtypeStruct((d, f), BF16), jax.ShapeDtypeStruct((f, d), BF16),
            jax.ShapeDtypeStruct((TAIL, d), F32)),
        in_specs=[whole, whole, whole, away, away],
        out_specs=(whole, whole, whole),
        scratch_shapes=scratch,
        compiler_params=pltpu.CompilerParams(
            collective_id=0, has_side_effects=True, vmem_limit_bytes=60000 * 1024),
    )(ext, meta8, head, weight_in[0], weight_out[0])
    tangent_home = jnp.tanh(tokens.astype(F32))
    dropped = (readout[None, :] * (1.0 - tangent_home * tangent_home)).astype(BF16)
    r2_grad = jnp.where((capacity_slot >= 0)[:, None], home[:pair].astype(BF16), dropped)
    return (r2_grad, grad_in[None], grad_out[None])


def solution(mesh, nx=4, cap=None):
    placed = (
        P(("dp", "expert"), None),
        P(("dp", "expert")),
        P(("dp", "expert")),
        P(("dp", "expert")),
        P(),
        P("dp", None, "expert"),
        P("dp", "expert", None),
    )
    return jax.shard_map(
        functools.partial(shards, nx, cap=cap),
        mesh=mesh,
        in_specs=placed,
        out_specs=(P(("dp", "expert"), None), P("dp", None, "expert"), P("dp", "expert", None)),
        check_vma=False,
    )
```

```python
import functools

import jax
import jax.numpy as jnp
from jax import lax
from jax.experimental import pallas as pl
from jax.experimental.pallas import tpu as pltpu
from jax.sharding import PartitionSpec as P

MESH = pl.DeviceIdType.MESH
F32 = jnp.float32
BF16 = jnp.bfloat16
BLK = 256
META = 128
SUB = 8
TAIL = 8


def dot(a, b, dims):
    return lax.dot_general(a, b, ((dims[:1], dims[1:]), ((), ())), preferred_element_type=F32)


def split_rows(tiles, parts):
    if tiles % parts or tiles // parts < 2:
        return (tiles,)
    first = (tiles // parts + 1) // 2 * parts
    return (first, tiles - first)


def far_first(n):
    return sorted(range(1, n), key=lambda k: (-min(k, n - k), k))


def drive(chains):
    chains = list(chains)
    while chains:
        for chain in list(chains):
            try:
                next(chain)
            except StopIteration:
                chains.remove(chain)


def kernel(cfg, ext_ref, meta_ref, head_ref, w1_hbm, w2_hbm, gin_ref, gout_ref, r2_ref, *scratch):
    nz, nx, ny, cap, batches = cfg
    (w1, w2, wsem, ssem, rsem, dr, ay, zs, zr, mr, rb, rpart, cbc, fb, hid, ts, tr, gi, go) = scratch[:19]
    per_batch = scratch[19:]
    n_own = len(per_batch) // len(batches)
    nb = 2 * nx
    rows = nz * cap
    tiles = rows // SUB
    nq = ny // 2
    capp = -(-cap // SUB) * SUB
    z = lax.axis_index("dp")
    j = lax.axis_index("expert")
    c = lax.rem(j, 2)
    y = lax.rem(j // 2, ny)
    x = j // (2 * ny)
    bid = 2 * x + c
    q, h = y // 2, lax.rem(y, 2)

    def at(px, py, pc):
        return {"expert": (px * ny + py) * 2 + pc}

    def ring(v, k, n):
        return lax.rem(v + k + n, n)

    partner = at(x, y, 1 - c)
    sends = []
    used = [0]

    def slots(n):
        base = used[0]
        used[0] += n
        return base

    def send(src, dst, sem, dev):
        copy = pltpu.make_async_remote_copy(
            src_ref=src, dst_ref=dst, send_sem=ssem.at[sem], recv_sem=rsem.at[sem],
            device_id=dev, device_id_type=MESH)
        copy.start()
        sends.append(copy)
        return copy

    w1_copy = pltpu.make_async_copy(w1_hbm, w1, wsem.at[0])
    w2_copy = pltpu.make_async_copy(w2_hbm, w2, wsem.at[1])
    w1_copy.start()
    w2_copy.start()

    barrier = pltpu.get_barrier_semaphore()
    peers = [{"dp": ring(z, k, nz)} for k in far_first(nz)]
    peers += [at(x, ring(y, k, ny), c) for k in far_first(ny)]
    peers += [at(ring(x, k, nx), y, pc) for k in far_first(nx) for pc in range(2)]
    peers += [partner]
    for dev in peers:
        pl.semaphore_signal(barrier, inc=1, device_id=dev, device_id_type=MESH)

    lane = lax.broadcasted_iota(jnp.int32, (ny * 2 * nb, nz * capp), 1)
    slot_id = jnp.full((ny * 2 * nb, nz * capp), -2, jnp.int32)
    for e in range(nz):
        inside = (lane >= e * capp) & (lane < e * capp + cap)
        slot_id = jnp.where(inside, lane - e * (capp - cap), slot_id)
    slot_id = slot_id.astype(F32)
    row_i = lax.broadcasted_iota(jnp.int32, (rows, nz * capp), 0)
    col_i = lax.broadcasted_iota(jnp.int32, (rows, nz * capp), 1)
    squeeze = jnp.zeros((rows, nz * capp), F32)
    for e in range(nz):
        inside = (col_i >= e * capp) & (col_i < e * capp + cap)
        squeeze = jnp.where(inside & (row_i == col_i - e * (capp - cap)), 1.0, squeeze)
    squeeze = squeeze.astype(BF16)

    pl.semaphore_wait(barrier, len(peers))

    base = slots(nb)
    got = []
    for k in far_first(nx) + [0]:
        for pc in range(2):
            if k == 0 and pc == 0:
                continue
            px, qc = ring(x, k, nx), lax.rem(c + pc, 2)
            i = 2 * k + pc
            got.append((i, send(ext_ref.at[2 * px + qc], dr.at[i], base + i, at(px, y, qc))))
    base = slots(nz)
    got_meta = [send(meta_ref, mr.at[z], base + k, {"dp": ring(z, k, nz)}) for k in far_first(nz)]
    mr[z] = meta_ref[...]

    width = BLK + META
    n_tok = ny * 2 * nb
    mine = ext_ref[bid].astype(F32)
    for i, copy in reversed(got):
        copy.wait_recv()
        mine = mine + dr[i].astype(F32)
    ay[y] = mine.astype(BF16)
    base = slots(ny)
    got = [send(ay.at[y], ay.at[y], base + k, at(x, ring(y, k, ny), c)) for k in far_first(ny)]
    for copy in got:
        copy.wait_recv()
    group = ay[...].reshape(n_tok, width)
    place = group[:, BLK:].astype(F32)[:, 0:1]
    onehot = jnp.where(place == slot_id, 1.0, 0.0).astype(BF16)
    packed = dot(onehot, group, (0, 0))
    zs[...] = packed.reshape(nz, capp // SUB, SUB, width).astype(BF16)

    base = slots(nz)
    got = [send(zs.at[ring(z, k, nz)], zr.at[z], base + k, {"dp": ring(z, k, nz)}) for k in far_first(nz)]
    zr[z] = zs[z]
    for copy in got:
        copy.wait_recv()
    spread = zr[...].astype(F32).reshape(nz * capp, width).astype(BF16)
    mine = dot(squeeze, spread, (1, 0))
    comb = mine[:, BLK + 1:BLK + 2]
    w1_copy.wait()
    w2_copy.wait()

    def cols(b):
        return pl.ds(pl.multiple_of(b * BLK, BLK), BLK)

    head = head_ref[2 * bid + h]
    ready = {}

    def chain(i):
        n_tiles = batches[i]
        first = sum(batches[:i])
        per_q = n_tiles // nq
        n = n_tiles * SUB
        here = slice(first * SUB, first * SUB + n)
        cs, cr, xs, xr, ys, yr, ab, ownf = per_batch[i * n_own:(i + 1) * n_own]
        comb_b = comb[here]

        def tiled(v):
            return [v[:, 128 * i:128 * (i + 1)].reshape(n_tiles, SUB, 128) for i in range(2)]

        def loaded(ref):
            return jnp.concatenate([ref[i].astype(F32).reshape(n, 128) for i in range(2)], axis=1)

        def store(ref, v):
            for i, p in enumerate(tiled(v)):
                ref[i] = p.astype(BF16)

        def spread_blocks(block, use):
            base = slots(nx)
            base2 = slots(nx)
            got = [(k, send(block(bid), block(bid), base + k, at(ring(x, k, nx), y, c))) for k in far_first(nx)]
            twin = [(0, send(block(bid), block(bid), base2, partner))]
            use(bid)
            yield
            for k, copy in reversed(got):
                copy.wait_recv()
                b = 2 * ring(x, -k, nx) + c
                twin.append((k, send(block(b), block(b), base2 + k, partner)))
                use(b)
            yield
            for k, copy in twin:
                copy.wait_recv()
                use(2 * ring(x, -k, nx) + 1 - c)

        def reduce_round(rd, part):
            base = slots(nx)
            base2 = slots(nx)
            base3 = slots(ny)
            order = far_first(nx) + [0]
            got = []
            for k in order:
                store(cs.at[rd, k], part(2 * ring(x, k, nx) + 1 - c))
                got.append(send(cs.at[rd, k], cr.at[rd, k], base + k, partner))
            parts = [part(2 * ring(x, k, nx) + c) for k in order]
            yield
            got_x = []
            for i, k in enumerate(order):
                got[i].wait_recv()
                v = parts[i] + loaded(cr.at[rd, k])
                if k:
                    store(xs.at[rd, k], v)
                    got_x.append((k, send(xs.at[rd, k], xr.at[rd, k], base2 + k, at(ring(x, k, nx), y, c))))
            yield
            for k, copy in reversed(got_x):
                copy.wait_recv()
                v = v + loaded(xr.at[rd, k])
            for i, p in enumerate(tiled(v)):
                ownf[i] = p
                ys[rd, i] = p.astype(BF16)
            got = []
            for k in far_first(ny):
                py = ring(y, k, ny)
                src = ys.at[rd, lax.rem(py, 2), pl.ds((py // 2) * per_q, per_q)]
                got.append((k, send(src, yr.at[rd, k], base3 + k, at(x, py, c))))
            total = ownf[h, pl.ds(q * per_q, per_q)]
            yield
            for k, copy in reversed(got):
                copy.wait_recv()
                total = total + yr[rd, k].astype(F32)
            return total

        def gather_round(rd, piece, use):
            ab[rd, bid, h, pl.ds(q * per_q, per_q)] = piece
            base = slots(ny)
            spot = ab.at[rd, bid, h, pl.ds(q * per_q, per_q)]
            got = [send(spot, spot, base + k, at(x, ring(y, k, ny), c)) for k in far_first(ny)]
            yield
            for copy in reversed(got):
                copy.wait_recv()

            def use_block(b):
                v = loaded(ab.at[rd, b]).astype(BF16)
                fb[rd, b, here] = v
                use(b, v)

            yield from spread_blocks(lambda b: ab.at[rd, b], use_block)

        acc = [jnp.zeros((n, w1.shape[0]), F32)]

        def use_rows(b):
            acc[0] = acc[0] + dot(rb[b, here], w1[:, cols(b)], (1, 1))

        rb[bid, here] = mine[here, :BLK].astype(BF16)
        cbc[first:first + n_tiles] = jnp.broadcast_to(comb_b, (n, 128)).reshape(n_tiles, SUB, 128)
        for i, p in enumerate(tiled(mine[here])):
            rpart[i, first:first + n_tiles] = p
        yield from spread_blocks(lambda b: rb.at[b, here], use_rows)
        pre = acc[0]
        sigm = jax.nn.sigmoid(pre)
        slope = sigm * (1.0 + pre * (1.0 - sigm))
        bend = sigm * (1.0 - sigm) * (2.0 + pre * (1.0 - 2.0 * sigm))
        hidden = (pre * sigm).astype(BF16)
        hid[0, here] = hidden
        r_piece = rpart[h, pl.ds(first + q * per_q, per_q)]
        c_piece = cbc[pl.ds(first + q * per_q, per_q)]

        mixed = yield from reduce_round(0, lambda b: comb_b * dot(hidden, w2[:, cols(b)], (1, 0)))
        tangent = jnp.tanh(r_piece + mixed)
        sech = 1.0 - tangent * tangent
        upstream = head * sech
        acc[0] = jnp.zeros_like(pre)

        def use_out(b, v):
            acc[0] = acc[0] + dot(v, w2[:, cols(b)], (1, 1))

        yield from gather_round(0, upstream.astype(BF16), use_out)
        back_hidden = comb_b * acc[0]
        back_pre = (back_hidden * slope).astype(BF16)
        hid[1, here] = back_pre

        grad = yield from reduce_round(1, lambda b: dot(back_pre, w1[:, cols(b)], (1, 0)))
        grad = (upstream + grad).astype(BF16)
        acc[0] = jnp.zeros_like(pre)

        def use_in(b, v):
            acc[0] = acc[0] + dot(v, w1[:, cols(b)], (1, 1))

        yield from gather_round(1, grad, use_in)
        second = acc[0]
        push = (comb_b * second * slope).astype(BF16)
        hid[2, here] = push
        ready[first] = True

        pushed = yield from reduce_round(2, lambda b: dot(push, w2[:, cols(b)], (1, 0)))
        curve = (grad.astype(F32) + pushed) * head * (-2.0 * tangent * sech)
        echo = (c_piece * curve).astype(BF16)
        acc[0] = jnp.zeros_like(pre)
        yield from gather_round(2, echo, use_out)
        hid[3, here] = (acc[0] * slope + second * back_hidden * bend).astype(BF16)

    base_tok = slots(nz)
    got_tok = []

    def fill():
        while len(ready) < len(batches):
            yield
        for copy in got_meta:
            copy.wait_recv()
        place = mr[...].astype(F32).reshape(nz * TAIL, META)[:, 0:1]
        home = lax.broadcasted_iota(jnp.int32, (nz * TAIL, 1), 0) // TAIL
        local = place - (z * cap).astype(F32)
        target = jnp.where((local >= 0.0) & (local < cap), local + (home * cap).astype(F32), -1.0)
        pick = lax.broadcasted_iota(jnp.int32, (nz * TAIL, rows), 1).astype(F32)
        pick = jnp.where(pick == target, 1.0, 0.0).astype(BF16)
        for b in range(nb):
            v = dot(pick, fb[1, b], (1, 0))
            ts[:, :, b * BLK:(b + 1) * BLK] = v.reshape(nz, TAIL, BLK).astype(BF16)
        for k in far_first(nz):
            pz = ring(z, k, nz)
            got_tok.append((k, send(ts.at[pz], tr.at[k], base_tok + k, {"dp": pz})))
        yield
        for b in range(nb):
            here = slice(b * BLK, (b + 1) * BLK)
            gi[:, here] = dot(hid[1], fb[1, b], (0, 0))
            go[:, here] = dot(hid[2], fb[0, b], (0, 0))
            if b % 2:
                yield

    drive([chain(i) for i in range(len(batches))] + [fill()])
    for b in range(nb):
        here = slice(b * BLK, (b + 1) * BLK)
        gin_ref[:, here] = (gi[:, here] + dot(hid[3], rb[b], (0, 0))).astype(BF16)
        gout_ref[:, here] = (go[:, here] + dot(hid[0], fb[2, b], (0, 0))).astype(BF16)
    home = ts[z].astype(F32)
    for k, copy in got_tok:
        copy.wait_recv()
        home = home + tr[k].astype(F32)
    r2_ref[...] = home
    for copy in sends:
        copy.wait_send()


def shards(nx, tokens, combine, routes, capacity_slot, readout, weight_in, weight_out, cap=None):
    nz = lax.axis_size("dp")
    ne = lax.axis_size("expert")
    ny = ne // (2 * nx)
    nb = 2 * nx
    pair, d = tokens.shape
    f = weight_in.shape[2]
    if cap is None:
        cap = 5 * pair * ne // (4 * nz)
    rows = nz * cap
    tiles = rows // SUB
    capp = -(-cap // SUB) * SUB
    batches = split_rows(tiles, ny // 2)
    width = BLK + META
    j = lax.axis_index("expert")
    spot = 2 * (j // (2 * ny)) + j % 2
    place = jnp.where(capacity_slot >= 0, routes * cap + capacity_slot, -1).astype(BF16)
    lane = lax.broadcasted_iota(jnp.int32, (pair, META), 1)
    meta = jnp.where(lane == 0, place[:, None], jnp.where(lane == 1, combine[:, None], 0)).astype(BF16)
    record = jnp.concatenate(
        [tokens.reshape(pair, nb, BLK).transpose(1, 0, 2), jnp.broadcast_to(meta[None], (nb, pair, META))], axis=2)
    row = lax.broadcasted_iota(jnp.int32, (1, nb * pair, 1), 1)
    ext = jnp.where(row // pair == spot, jnp.tile(record, (1, nb, 1)), 0).astype(BF16)
    meta8 = jnp.pad(meta, ((0, TAIL - pair), (0, 0)), constant_values=-1)
    head = readout.reshape(2 * nb, 1, 128)
    vm = pltpu.VMEM
    n_sem = nb + 3 * nz + ny + len(batches) * (2 * nx + 3 * (4 * nx + 2 * ny))
    scratch = [
        vm((f, d), BF16), vm((f, d), BF16), pltpu.SemaphoreType.DMA((2,)),
        pltpu.SemaphoreType.DMA((n_sem,)), pltpu.SemaphoreType.DMA((n_sem,)),
        vm((nb, nb * pair, width), BF16), vm((ny, nb * pair, width), BF16),
        vm((nz, capp // SUB, SUB, width), BF16), vm((nz, capp // SUB, SUB, width), BF16),
        vm((nz, TAIL, META), BF16),
        vm((nb, rows, BLK), BF16), vm((2, tiles, SUB, 128), F32), vm((tiles, SUB, 128), F32),
        vm((3, nb, rows, BLK), BF16), vm((4, rows, f), BF16),
        vm((nz, TAIL, d), BF16), vm((nz, TAIL, d), BF16), vm((f, d), F32), vm((f, d), F32),
    ]
    for n in batches:
        scratch += [vm((3, nx, 2, n, SUB, 128), BF16)] * 4
        scratch += [vm((3, 2, n, SUB, 128), BF16), vm((3, ny, 2 * n // ny, SUB, 128), BF16)]
        scratch += [vm((3, nb, 2, n, SUB, 128), BF16), vm((2, n, SUB, 128), F32)]
    whole = pl.BlockSpec(memory_space=pltpu.VMEM)
    away = pl.BlockSpec(memory_space=pl.ANY)
    grad_in, grad_out, home = pl.pallas_call(
        functools.partial(kernel, (nz, nx, ny, cap, batches)),
        out_shape=(
            jax.ShapeDtypeStruct((f, d), BF16), jax.ShapeDtypeStruct((f, d), BF16),
            jax.ShapeDtypeStruct((TAIL, d), F32)),
        in_specs=[whole, whole, whole, away, away],
        out_specs=(whole, whole, whole),
        scratch_shapes=scratch,
        compiler_params=pltpu.CompilerParams(
            collective_id=0, has_side_effects=True, vmem_limit_bytes=60000 * 1024),
    )(ext, meta8, head, weight_in[0].T, weight_out[0])
    tangent_home = jnp.tanh(tokens.astype(F32))
    dropped = (readout[None, :] * (1.0 - tangent_home * tangent_home)).astype(BF16)
    r2_grad = jnp.where((capacity_slot >= 0)[:, None], home[:pair].astype(BF16), dropped)
    return (r2_grad, grad_in.T[None], grad_out[None])


def solution(mesh, nx=4, cap=None):
    placed = (
        P(("dp", "expert"), None),
        P(("dp", "expert")),
        P(("dp", "expert")),
        P(("dp", "expert")),
        P(),
        P("dp", None, "expert"),
        P("dp", "expert", None),
    )
    return jax.shard_map(
        functools.partial(shards, nx, cap=cap),
        mesh=mesh,
        in_specs=placed,
        out_specs=(P(("dp", "expert"), None), P("dp", None, "expert"), P("dp", "expert", None)),
        check_vma=False,
    )
```

```python
import functools

import jax
import jax.numpy as jnp
from jax import lax
from jax.experimental import pallas as pl
from jax.experimental.pallas import tpu as pltpu
from jax.sharding import PartitionSpec as P

MESH = pl.DeviceIdType.MESH
F32 = jnp.float32
BF16 = jnp.bfloat16
BLK = 256
META = 128
SUB = 8
TAIL = 8


def dot(a, b, dims):
    return lax.dot_general(a, b, ((dims[:1], dims[1:]), ((), ())), preferred_element_type=F32)


def split_rows(tiles, parts):
    if tiles % parts or tiles // parts < 2:
        return (tiles,)
    first = (tiles // parts + 1) // 2 * parts
    return (first, tiles - first)


def far_first(n):
    return sorted(range(1, n), key=lambda k: (-min(k, n - k), k))


def drive(chains):
    chains = list(chains)
    while chains:
        for chain in list(chains):
            try:
                next(chain)
            except StopIteration:
                chains.remove(chain)


def finish(slot_ref, gin_in, gout_in, home_ref, tok_ref, head_ref, gin_ref, gout_ref, r2_ref):
    gin_ref[...] = gin_in[...]
    gout_ref[...] = gout_in[...]
    tangent = jnp.tanh(tok_ref[...].astype(F32))
    dropped = (head_ref[...] * (1.0 - tangent * tangent)).astype(BF16)
    odd = lax.broadcasted_iota(jnp.int32, tangent.shape, 0) == 1
    slot = jnp.where(odd, slot_ref[1], slot_ref[0])
    picked = home_ref[0:2, :].astype(BF16)
    r2_ref[...] = jnp.where(slot >= 0, picked.astype(F32), dropped.astype(F32)).astype(BF16)


def kernel(cfg, routes_ref, slot_ref, comb_ref, tok_ref, head_ref, w1_hbm, w2_hbm, gin_ref, gout_ref, r2_ref, *scratch):
    nz, nx, ny, cap, batches = cfg
    (w1, w2, wsem, ssem, rsem, dr, ay, zs, zr, mr, rb, rpart, cbc, fb, hid, ts, tr, gi, go, ext_ref, meta_ref) = scratch[:21]
    per_batch = scratch[21:]
    n_own = len(per_batch) // len(batches)
    nb = 2 * nx
    rows = nz * cap
    tiles = rows // SUB
    nq = ny // 2
    capp = -(-cap // SUB) * SUB
    z = lax.axis_index("dp")
    j = lax.axis_index("expert")
    c = lax.rem(j, 2)
    y = lax.rem(j // 2, ny)
    x = j // (2 * ny)
    bid = 2 * x + c
    q, h = y // 2, lax.rem(y, 2)

    def at(px, py, pc):
        return {"expert": (px * ny + py) * 2 + pc}

    def ring(v, k, n):
        return lax.rem(v + k + n, n)

    partner = at(x, y, 1 - c)
    sends = []
    used = [0]

    def slots(n):
        base = used[0]
        used[0] += n
        return base

    def send(src, dst, sem, dev):
        copy = pltpu.make_async_remote_copy(
            src_ref=src, dst_ref=dst, send_sem=ssem.at[sem], recv_sem=rsem.at[sem],
            device_id=dev, device_id_type=MESH)
        copy.start()
        sends.append(copy)
        return copy

    w1_copy = pltpu.make_async_copy(w1_hbm, w1, wsem.at[0])
    w2_copy = pltpu.make_async_copy(w2_hbm, w2, wsem.at[1])
    w1_copy.start()
    w2_copy.start()

    barrier = pltpu.get_barrier_semaphore()
    peers = [{"dp": ring(z, k, nz)} for k in far_first(nz)]
    peers += [at(x, ring(y, k, ny), c) for k in far_first(ny)]
    peers += [at(ring(x, k, nx), y, pc) for k in far_first(nx) for pc in range(2)]
    peers += [partner]
    for dev in peers:
        pl.semaphore_signal(barrier, inc=1, device_id=dev, device_id_type=MESH)

    places = [jnp.where(slot_ref[i] >= 0, routes_ref[i] * cap + slot_ref[i], -1).astype(F32) for i in range(2)]
    weight = comb_ref[...].astype(F32)

    def token_meta(n):
        row = lax.broadcasted_iota(jnp.int32, (n, META), 0)
        lane = lax.broadcasted_iota(jnp.int32, (n, META), 1)
        odd = lax.rem(row, 2) == 1
        place = jnp.where(odd, places[1], places[0])
        own = jnp.where(odd, jnp.broadcast_to(weight[:, 1:2], (n, META)), jnp.broadcast_to(weight[:, 0:1], (n, META)))
        return row, jnp.where(lane == 0, place, jnp.where(lane == 1, own, 0.0))

    row, meta = token_meta(TAIL)
    meta_ref[...] = jnp.where(row < 2, meta, -1.0).astype(BF16)
    row, meta = token_meta(2 * nb)
    meta = jnp.where(row // 2 == bid, meta, 0.0).astype(BF16)
    row = lax.broadcasted_iota(jnp.int32, (2 * nb, BLK), 0)
    for b in range(nb):
        pair = tok_ref[:, b * BLK:(b + 1) * BLK].astype(F32)
        v = jnp.where(lax.rem(row, 2) == 1, jnp.broadcast_to(pair[1:2], row.shape), jnp.broadcast_to(pair[0:1], row.shape))
        ext_ref[b, :, :BLK] = jnp.where(row // 2 == bid, v, 0.0).astype(BF16)
        ext_ref[b, :, BLK:] = meta

    lane = lax.broadcasted_iota(jnp.int32, (ny * 2 * nb, nz * capp), 1)
    slot_id = jnp.full((ny * 2 * nb, nz * capp), -2, jnp.int32)
    for e in range(nz):
        inside = (lane >= e * capp) & (lane < e * capp + cap)
        slot_id = jnp.where(inside, lane - e * (capp - cap), slot_id)
    slot_id = slot_id.astype(F32)
    row_i = lax.broadcasted_iota(jnp.int32, (rows, nz * capp), 0)
    col_i = lax.broadcasted_iota(jnp.int32, (rows, nz * capp), 1)
    squeeze = jnp.zeros((rows, nz * capp), F32)
    for e in range(nz):
        inside = (col_i >= e * capp) & (col_i < e * capp + cap)
        squeeze = jnp.where(inside & (row_i == col_i - e * (capp - cap)), 1.0, squeeze)
    squeeze = squeeze.astype(BF16)

    pl.semaphore_wait(barrier, len(peers))

    base = slots(nb)
    got = []
    for k in far_first(nx) + [0]:
        for pc in range(2):
            if k == 0 and pc == 0:
                continue
            px, qc = ring(x, k, nx), lax.rem(c + pc, 2)
            i = 2 * k + pc
            got.append((i, send(ext_ref.at[2 * px + qc], dr.at[i], base + i, at(px, y, qc))))
    base = slots(nz)
    got_meta = [send(meta_ref, mr.at[z], base + k, {"dp": ring(z, k, nz)}) for k in far_first(nz)]
    mr[z] = meta_ref[...]

    width = BLK + META
    n_tok = ny * 2 * nb
    mine = ext_ref[bid].astype(F32)
    for i, copy in reversed(got):
        copy.wait_recv()
        mine = mine + dr[i].astype(F32)
    ay[y] = mine.astype(BF16)
    base = slots(ny)
    got = [send(ay.at[y], ay.at[y], base + k, at(x, ring(y, k, ny), c)) for k in far_first(ny)]
    for copy in got:
        copy.wait_recv()
    group = ay[...].reshape(n_tok, width)
    place = group[:, BLK:].astype(F32)[:, 0:1]
    onehot = jnp.where(place == slot_id, 1.0, 0.0).astype(BF16)
    packed = dot(onehot, group, (0, 0))
    zs[...] = packed.reshape(nz, capp // SUB, SUB, width).astype(BF16)

    base = slots(nz)
    got = [send(zs.at[ring(z, k, nz)], zr.at[z], base + k, {"dp": ring(z, k, nz)}) for k in far_first(nz)]
    zr[z] = zs[z]
    for copy in got:
        copy.wait_recv()
    spread = zr[...].astype(F32).reshape(nz * capp, width).astype(BF16)
    mine = dot(squeeze, spread, (1, 0))
    comb = mine[:, BLK + 1:BLK + 2]
    w1_copy.wait()
    w2_copy.wait()

    def cols(b):
        return pl.ds(pl.multiple_of(b * BLK, BLK), BLK)

    head = head_ref[2 * bid + h]
    ready = {}

    def chain(i):
        n_tiles = batches[i]
        first = sum(batches[:i])
        per_q = n_tiles // nq
        n = n_tiles * SUB
        here = slice(first * SUB, first * SUB + n)
        cs, cr, xs, xr, ys, yr, ab, ownf = per_batch[i * n_own:(i + 1) * n_own]
        comb_b = comb[here]

        def tiled(v):
            return [v[:, 128 * i:128 * (i + 1)].reshape(n_tiles, SUB, 128) for i in range(2)]

        def loaded(ref):
            return jnp.concatenate([ref[i].astype(F32).reshape(n, 128) for i in range(2)], axis=1)

        def store(ref, v):
            for i, p in enumerate(tiled(v)):
                ref[i] = p.astype(BF16)

        def spread_blocks(block, use):
            base = slots(nx)
            base2 = slots(nx)
            got = [(k, send(block(bid), block(bid), base + k, at(ring(x, k, nx), y, c))) for k in far_first(nx)]
            twin = [(0, send(block(bid), block(bid), base2, partner))]
            use(bid)
            yield
            for k, copy in reversed(got):
                copy.wait_recv()
                b = 2 * ring(x, -k, nx) + c
                twin.append((k, send(block(b), block(b), base2 + k, partner)))
                use(b)
            yield
            for k, copy in twin:
                copy.wait_recv()
                use(2 * ring(x, -k, nx) + 1 - c)

        def reduce_round(rd, part):
            base = slots(nx)
            base2 = slots(nx)
            base3 = slots(ny)
            order = far_first(nx) + [0]
            got = []
            for k in order:
                store(cs.at[rd, k], part(2 * ring(x, k, nx) + 1 - c))
                got.append(send(cs.at[rd, k], cr.at[rd, k], base + k, partner))
            parts = [part(2 * ring(x, k, nx) + c) for k in order]
            yield
            got_x = []
            for i, k in enumerate(order):
                got[i].wait_recv()
                v = parts[i] + loaded(cr.at[rd, k])
                if k:
                    store(xs.at[rd, k], v)
                    got_x.append((k, send(xs.at[rd, k], xr.at[rd, k], base2 + k, at(ring(x, k, nx), y, c))))
            yield
            for k, copy in reversed(got_x):
                copy.wait_recv()
                v = v + loaded(xr.at[rd, k])
            for i, p in enumerate(tiled(v)):
                ownf[i] = p
                ys[rd, i] = p.astype(BF16)
            got = []
            for k in far_first(ny):
                py = ring(y, k, ny)
                src = ys.at[rd, lax.rem(py, 2), pl.ds((py // 2) * per_q, per_q)]
                got.append((k, send(src, yr.at[rd, k], base3 + k, at(x, py, c))))
            total = ownf[h, pl.ds(q * per_q, per_q)]
            yield
            for k, copy in reversed(got):
                copy.wait_recv()
                total = total + yr[rd, k].astype(F32)
            return total

        def gather_round(rd, piece, use):
            ab[rd, bid, h, pl.ds(q * per_q, per_q)] = piece
            base = slots(ny)
            spot = ab.at[rd, bid, h, pl.ds(q * per_q, per_q)]
            got = [send(spot, spot, base + k, at(x, ring(y, k, ny), c)) for k in far_first(ny)]
            yield
            for copy in reversed(got):
                copy.wait_recv()

            def use_block(b):
                v = loaded(ab.at[rd, b]).astype(BF16)
                fb[rd, b, here] = v
                use(b, v)

            yield from spread_blocks(lambda b: ab.at[rd, b], use_block)

        acc = [jnp.zeros((n, w1.shape[0]), F32)]

        def use_rows(b):
            acc[0] = acc[0] + dot(rb[b, here], w1[:, cols(b)], (1, 1))

        rb[bid, here] = mine[here, :BLK].astype(BF16)
        cbc[first:first + n_tiles] = jnp.broadcast_to(comb_b, (n, 128)).reshape(n_tiles, SUB, 128)
        for i, p in enumerate(tiled(mine[here])):
            rpart[i, first:first + n_tiles] = p
        yield from spread_blocks(lambda b: rb.at[b, here], use_rows)
        pre = acc[0]
        sigm = jax.nn.sigmoid(pre)
        slope = sigm * (1.0 + pre * (1.0 - sigm))
        bend = sigm * (1.0 - sigm) * (2.0 + pre * (1.0 - 2.0 * sigm))
        hidden = (pre * sigm).astype(BF16)
        hid[0, here] = hidden
        r_piece = rpart[h, pl.ds(first + q * per_q, per_q)]
        c_piece = cbc[pl.ds(first + q * per_q, per_q)]

        mixed = yield from reduce_round(0, lambda b: comb_b * dot(hidden, w2[:, cols(b)], (1, 0)))
        tangent = jnp.tanh(r_piece + mixed)
        sech = 1.0 - tangent * tangent
        upstream = head * sech
        acc[0] = jnp.zeros_like(pre)

        def use_out(b, v):
            acc[0] = acc[0] + dot(v, w2[:, cols(b)], (1, 1))

        yield from gather_round(0, upstream.astype(BF16), use_out)
        back_hidden = comb_b * acc[0]
        back_pre = (back_hidden * slope).astype(BF16)
        hid[1, here] = back_pre

        grad = yield from reduce_round(1, lambda b: dot(back_pre, w1[:, cols(b)], (1, 0)))
        grad = (upstream + grad).astype(BF16)
        acc[0] = jnp.zeros_like(pre)

        def use_in(b, v):
            acc[0] = acc[0] + dot(v, w1[:, cols(b)], (1, 1))

        yield from gather_round(1, grad, use_in)
        second = acc[0]
        push = (comb_b * second * slope).astype(BF16)
        hid[2, here] = push
        ready[first] = True

        pushed = yield from reduce_round(2, lambda b: dot(push, w2[:, cols(b)], (1, 0)))
        curve = (grad.astype(F32) + pushed) * head * (-2.0 * tangent * sech)
        echo = (c_piece * curve).astype(BF16)
        acc[0] = jnp.zeros_like(pre)
        yield from gather_round(2, echo, use_out)
        hid[3, here] = (acc[0] * slope + second * back_hidden * bend).astype(BF16)

    base_tok = slots(nz)
    got_tok = []

    def fill():
        while len(ready) < len(batches):
            yield
        for copy in got_meta:
            copy.wait_recv()
        place = mr[...].astype(F32).reshape(nz * TAIL, META)[:, 0:1]
        home = lax.broadcasted_iota(jnp.int32, (nz * TAIL, 1), 0) // TAIL
        local = place - (z * cap).astype(F32)
        target = jnp.where((local >= 0.0) & (local < cap), local + (home * cap).astype(F32), -1.0)
        pick = lax.broadcasted_iota(jnp.int32, (nz * TAIL, rows), 1).astype(F32)
        pick = jnp.where(pick == target, 1.0, 0.0).astype(BF16)
        for b in range(nb):
            v = dot(pick, fb[1, b], (1, 0))
            ts[:, :, b * BLK:(b + 1) * BLK] = v.reshape(nz, TAIL, BLK).astype(BF16)
        for k in far_first(nz):
            pz = ring(z, k, nz)
            got_tok.append((k, send(ts.at[pz], tr.at[k], base_tok + k, {"dp": pz})))
        yield
        for b in range(nb):
            here = slice(b * BLK, (b + 1) * BLK)
            gi[:, here] = dot(hid[1], fb[1, b], (0, 0))
            go[:, here] = dot(hid[2], fb[0, b], (0, 0))
            if b % 2:
                yield

    drive([chain(i) for i in range(len(batches))] + [fill()])
    for b in range(nb):
        here = slice(b * BLK, (b + 1) * BLK)
        gin_ref[:, here] = (gi[:, here] + dot(hid[3], rb[b], (0, 0))).astype(BF16)
        gout_ref[:, here] = (go[:, here] + dot(hid[0], fb[2, b], (0, 0))).astype(BF16)
    home = ts[z].astype(F32)
    for k, copy in got_tok:
        copy.wait_recv()
        home = home + tr[k].astype(F32)
    r2_ref[...] = home
    for copy in sends:
        copy.wait_send()


def shards(nx, tokens, combine, routes, capacity_slot, readout, weight_in, weight_out, cap=None):
    nz = lax.axis_size("dp")
    ne = lax.axis_size("expert")
    ny = ne // (2 * nx)
    nb = 2 * nx
    pair, d = tokens.shape
    f = weight_in.shape[2]
    if cap is None:
        cap = 5 * pair * ne // (4 * nz)
    rows = nz * cap
    tiles = rows // SUB
    capp = -(-cap // SUB) * SUB
    batches = split_rows(tiles, ny // 2)
    width = BLK + META
    head = readout.reshape(2 * nb, 1, 128)
    vm = pltpu.VMEM
    n_sem = nb + 3 * nz + ny + len(batches) * (2 * nx + 3 * (4 * nx + 2 * ny))
    scratch = [
        vm((f, d), BF16), vm((f, d), BF16), pltpu.SemaphoreType.DMA((2,)),
        pltpu.SemaphoreType.DMA((n_sem,)), pltpu.SemaphoreType.DMA((n_sem,)),
        vm((nb, nb * pair, width), BF16), vm((ny, nb * pair, width), BF16),
        vm((nz, capp // SUB, SUB, width), BF16), vm((nz, capp // SUB, SUB, width), BF16),
        vm((nz, TAIL, META), BF16),
        vm((nb, rows, BLK), BF16), vm((2, tiles, SUB, 128), F32), vm((tiles, SUB, 128), F32),
        vm((3, nb, rows, BLK), BF16), vm((4, rows, f), BF16),
        vm((nz, TAIL, d), BF16), vm((nz, TAIL, d), BF16), vm((f, d), F32), vm((f, d), F32),
        vm((nb, nb * pair, width), BF16), vm((TAIL, META), BF16),
    ]
    for n in batches:
        scratch += [vm((3, nx, 2, n, SUB, 128), BF16)] * 4
        scratch += [vm((3, 2, n, SUB, 128), BF16), vm((3, ny, 2 * n // ny, SUB, 128), BF16)]
        scratch += [vm((3, nb, 2, n, SUB, 128), BF16), vm((2, n, SUB, 128), F32)]
    whole = pl.BlockSpec(memory_space=pltpu.VMEM)
    away = pl.BlockSpec(memory_space=pl.ANY)
    scalars = pl.BlockSpec(memory_space=pltpu.SMEM)
    grad_in, grad_out, home = pl.pallas_call(
        functools.partial(kernel, (nz, nx, ny, cap, batches)),
        out_shape=(
            jax.ShapeDtypeStruct((f, d), BF16), jax.ShapeDtypeStruct((f, d), BF16),
            jax.ShapeDtypeStruct((TAIL, d), F32)),
        in_specs=[scalars, scalars, whole, whole, whole, away, away],
        out_specs=(whole, whole, whole),
        scratch_shapes=scratch,
        compiler_params=pltpu.CompilerParams(
            collective_id=0, has_side_effects=True, vmem_limit_bytes=60000 * 1024),
    )(routes, capacity_slot, combine.reshape(1, pair), tokens, head, weight_in[0].T, weight_out[0])
    steps = 4
    part = d // steps

    def slab(n):
        return pl.BlockSpec((n, part), lambda i: (0, i))

    grad_in, grad_out, r2_grad = pl.pallas_call(
        finish,
        grid=(steps,),
        out_shape=(
            jax.ShapeDtypeStruct((f, d), BF16), jax.ShapeDtypeStruct((f, d), BF16),
            jax.ShapeDtypeStruct((pair, d), BF16)),
        in_specs=[scalars, slab(f), slab(f), slab(TAIL), slab(pair), slab(1)],
        out_specs=(slab(f), slab(f), slab(pair)),
    )(capacity_slot, grad_in, grad_out, home, tokens, readout.reshape(1, d))
    return (r2_grad, grad_in.T[None], grad_out[None])


def solution(mesh, nx=4, cap=None):
    placed = (
        P(("dp", "expert"), None),
        P(("dp", "expert")),
        P(("dp", "expert")),
        P(("dp", "expert")),
        P(),
        P("dp", None, "expert"),
        P("dp", "expert", None),
    )
    return jax.shard_map(
        functools.partial(shards, nx, cap=cap),
        mesh=mesh,
        in_specs=placed,
        out_specs=(P(("dp", "expert"), None), P("dp", None, "expert"), P("dp", "expert", None)),
        check_vma=False,
    )
```

```python
import functools

import jax
import jax.numpy as jnp
from jax import lax
from jax.experimental import pallas as pl
from jax.experimental.pallas import tpu as pltpu
from jax.sharding import PartitionSpec as P

MESH = pl.DeviceIdType.MESH
F32 = jnp.float32
BF16 = jnp.bfloat16
BLK = 256
META = 128
SUB = 8
TAIL = 8


def dot(a, b, dims):
    return lax.dot_general(a, b, ((dims[:1], dims[1:]), ((), ())), preferred_element_type=F32)


def split_rows(tiles, parts):
    if tiles % parts or tiles // parts < 2:
        return (tiles,)
    first = tiles // parts // 2 * parts
    return (first, tiles - first)


def far_first(n):
    return sorted(range(1, n), key=lambda k: (-min(k, n - k), k))


def drive(chains):
    chains = list(chains)
    while chains:
        for chain in list(chains):
            try:
                next(chain)
            except StopIteration:
                chains.remove(chain)


def finish(slot_ref, gin_in, gout_in, home_ref, tok_ref, head_ref, gin_ref, gout_ref, r2_ref):
    gin_ref[...] = gin_in[...]
    gout_ref[...] = gout_in[...]
    tangent = jnp.tanh(tok_ref[...].astype(F32))
    dropped = (head_ref[...] * (1.0 - tangent * tangent)).astype(BF16)
    odd = lax.broadcasted_iota(jnp.int32, tangent.shape, 0) == 1
    slot = jnp.where(odd, slot_ref[1], slot_ref[0])
    picked = home_ref[0:2, :].astype(BF16)
    r2_ref[...] = jnp.where(slot >= 0, picked.astype(F32), dropped.astype(F32)).astype(BF16)


def kernel(cfg, routes_ref, slot_ref, comb_ref, tok_ref, head_ref, w1_hbm, w2_hbm, gin_ref, gout_ref, r2_ref, *scratch):
    nz, nx, ny, cap, batches = cfg
    (w1, w2, wsem, ssem, rsem, dr, ay, zs, zr, mr, rb, rpart, cbc, fb, hid, ts, tr, gi, go, ext_ref, meta_ref) = scratch[:21]
    per_batch = scratch[21:]
    n_own = len(per_batch) // len(batches)
    nb = 2 * nx
    rows = nz * cap
    tiles = rows // SUB
    nq = ny // 2
    capp = -(-cap // SUB) * SUB
    z = lax.axis_index("dp")
    j = lax.axis_index("expert")
    c = lax.rem(j, 2)
    y = lax.rem(j // 2, ny)
    x = j // (2 * ny)
    bid = 2 * x + c
    q, h = y // 2, lax.rem(y, 2)

    def at(px, py, pc):
        return {"expert": (px * ny + py) * 2 + pc}

    def ring(v, k, n):
        return lax.rem(v + k + n, n)

    partner = at(x, y, 1 - c)
    sends = []
    used = [0]

    def slots(n):
        base = used[0]
        used[0] += n
        return base

    def send(src, dst, sem, dev):
        copy = pltpu.make_async_remote_copy(
            src_ref=src, dst_ref=dst, send_sem=ssem.at[sem], recv_sem=rsem.at[sem],
            device_id=dev, device_id_type=MESH)
        copy.start()
        sends.append(copy)
        return copy

    w1_copy = pltpu.make_async_copy(w1_hbm, w1, wsem.at[0])
    w2_copy = pltpu.make_async_copy(w2_hbm, w2, wsem.at[1])
    w1_copy.start()
    w2_copy.start()

    barrier = pltpu.get_barrier_semaphore()
    peers = [{"dp": ring(z, k, nz)} for k in far_first(nz)]
    peers += [at(x, ring(y, k, ny), c) for k in far_first(ny)]
    peers += [at(ring(x, k, nx), y, pc) for k in far_first(nx) for pc in range(2)]
    peers += [partner]
    for dev in peers:
        pl.semaphore_signal(barrier, inc=1, device_id=dev, device_id_type=MESH)

    places = [jnp.where(slot_ref[i] >= 0, routes_ref[i] * cap + slot_ref[i], -1).astype(F32) for i in range(2)]
    weight = comb_ref[...].astype(F32)

    def token_meta(n):
        row = lax.broadcasted_iota(jnp.int32, (n, META), 0)
        lane = lax.broadcasted_iota(jnp.int32, (n, META), 1)
        odd = lax.rem(row, 2) == 1
        place = jnp.where(odd, places[1], places[0])
        own = jnp.where(odd, jnp.broadcast_to(weight[:, 1:2], (n, META)), jnp.broadcast_to(weight[:, 0:1], (n, META)))
        return row, jnp.where(lane == 0, place, jnp.where(lane == 1, own, 0.0))

    row, meta = token_meta(TAIL)
    meta_ref[...] = jnp.where(row < 2, meta, -1.0).astype(BF16)
    row, meta = token_meta(2 * nb)
    meta = jnp.where(row // 2 == bid, meta, 0.0).astype(BF16)
    row = lax.broadcasted_iota(jnp.int32, (2 * nb, BLK), 0)
    for b in range(nb):
        pair = tok_ref[:, b * BLK:(b + 1) * BLK].astype(F32)
        v = jnp.where(lax.rem(row, 2) == 1, jnp.broadcast_to(pair[1:2], row.shape), jnp.broadcast_to(pair[0:1], row.shape))
        ext_ref[b, :, :BLK] = jnp.where(row // 2 == bid, v, 0.0).astype(BF16)
        ext_ref[b, :, BLK:] = meta

    lane = lax.broadcasted_iota(jnp.int32, (ny * 2 * nb, nz * capp), 1)
    slot_id = jnp.full((ny * 2 * nb, nz * capp), -2, jnp.int32)
    for e in range(nz):
        inside = (lane >= e * capp) & (lane < e * capp + cap)
        slot_id = jnp.where(inside, lane - e * (capp - cap), slot_id)
    slot_id = slot_id.astype(F32)
    row_i = lax.broadcasted_iota(jnp.int32, (rows, nz * capp), 0)
    col_i = lax.broadcasted_iota(jnp.int32, (rows, nz * capp), 1)
    squeeze = jnp.zeros((rows, nz * capp), F32)
    for e in range(nz):
        inside = (col_i >= e * capp) & (col_i < e * capp + cap)
        squeeze = jnp.where(inside & (row_i == col_i - e * (capp - cap)), 1.0, squeeze)
    squeeze = squeeze.astype(BF16)

    pl.semaphore_wait(barrier, len(peers))

    base = slots(nb)
    got = []
    for k in far_first(nx) + [0]:
        for pc in range(2):
            if k == 0 and pc == 0:
                continue
            px, qc = ring(x, k, nx), lax.rem(c + pc, 2)
            i = 2 * k + pc
            got.append((i, send(ext_ref.at[2 * px + qc], dr.at[i], base + i, at(px, y, qc))))
    base = slots(nz)
    got_meta = [send(meta_ref, mr.at[z], base + k, {"dp": ring(z, k, nz)}) for k in far_first(nz)]
    mr[z] = meta_ref[...]

    width = BLK + META
    n_tok = ny * 2 * nb
    mine = ext_ref[bid].astype(F32)
    for i, copy in reversed(got):
        copy.wait_recv()
        mine = mine + dr[i].astype(F32)
    ay[y] = mine.astype(BF16)
    base = slots(ny)
    got = [send(ay.at[y], ay.at[y], base + k, at(x, ring(y, k, ny), c)) for k in far_first(ny)]
    for copy in got:
        copy.wait_recv()
    group = ay[...].reshape(n_tok, width)
    place = group[:, BLK:].astype(F32)[:, 0:1]
    onehot = jnp.where(place == slot_id, 1.0, 0.0).astype(BF16)
    packed = dot(onehot, group, (0, 0))
    zs[...] = packed.reshape(nz, capp // SUB, SUB, width).astype(BF16)

    base = slots(nz)
    got = [send(zs.at[ring(z, k, nz)], zr.at[z], base + k, {"dp": ring(z, k, nz)}) for k in far_first(nz)]
    zr[z] = zs[z]
    for copy in got:
        copy.wait_recv()
    spread = zr[...].astype(F32).reshape(nz * capp, width).astype(BF16)
    mine = dot(squeeze, spread, (1, 0))
    comb = mine[:, BLK + 1:BLK + 2]
    w1_copy.wait()
    w2_copy.wait()

    def cols(b):
        return pl.ds(pl.multiple_of(b * BLK, BLK), BLK)

    head = head_ref[2 * bid + h]
    ready = {}

    def chain(i):
        n_tiles = batches[i]
        first = sum(batches[:i])
        per_q = n_tiles // nq
        n = n_tiles * SUB
        here = slice(first * SUB, first * SUB + n)
        cs, cr, xs, xr, ys, yr, ab, ownf = per_batch[i * n_own:(i + 1) * n_own]
        comb_b = comb[here]

        def tiled(v):
            return [v[:, 128 * i:128 * (i + 1)].reshape(n_tiles, SUB, 128) for i in range(2)]

        def loaded(ref):
            return jnp.concatenate([ref[i].astype(F32).reshape(n, 128) for i in range(2)], axis=1)

        def store(ref, v):
            for i, p in enumerate(tiled(v)):
                ref[i] = p.astype(BF16)

        def spread_blocks(block, use):
            base = slots(nx)
            base2 = slots(nx)
            got = [(k, send(block(bid), block(bid), base + k, at(ring(x, k, nx), y, c))) for k in far_first(nx)]
            twin = [(0, send(block(bid), block(bid), base2, partner))]
            use(bid)
            yield
            for k, copy in reversed(got):
                copy.wait_recv()
                b = 2 * ring(x, -k, nx) + c
                twin.append((k, send(block(b), block(b), base2 + k, partner)))
                use(b)
            yield
            for k, copy in twin:
                copy.wait_recv()
                use(2 * ring(x, -k, nx) + 1 - c)

        def reduce_round(rd, part):
            base = slots(nx)
            base2 = slots(nx)
            base3 = slots(ny)
            order = far_first(nx) + [0]
            got = []
            for k in order:
                store(cs.at[rd, k], part(2 * ring(x, k, nx) + 1 - c))
                got.append(send(cs.at[rd, k], cr.at[rd, k], base + k, partner))
            parts = [part(2 * ring(x, k, nx) + c) for k in order]
            yield
            got_x = []
            for i, k in enumerate(order):
                got[i].wait_recv()
                v = parts[i] + loaded(cr.at[rd, k])
                if k:
                    store(xs.at[rd, k], v)
                    got_x.append((k, send(xs.at[rd, k], xr.at[rd, k], base2 + k, at(ring(x, k, nx), y, c))))
            yield
            for k, copy in reversed(got_x):
                copy.wait_recv()
                v = v + loaded(xr.at[rd, k])
            for i, p in enumerate(tiled(v)):
                ownf[i] = p
                ys[rd, i] = p.astype(BF16)
            got = []
            for k in far_first(ny):
                py = ring(y, k, ny)
                src = ys.at[rd, lax.rem(py, 2), pl.ds((py // 2) * per_q, per_q)]
                got.append((k, send(src, yr.at[rd, k], base3 + k, at(x, py, c))))
            total = ownf[h, pl.ds(q * per_q, per_q)]
            yield
            for k, copy in reversed(got):
                copy.wait_recv()
                total = total + yr[rd, k].astype(F32)
            return total

        def gather_round(rd, piece, use):
            ab[rd, bid, h, pl.ds(q * per_q, per_q)] = piece
            base = slots(ny)
            spot = ab.at[rd, bid, h, pl.ds(q * per_q, per_q)]
            got = [send(spot, spot, base + k, at(x, ring(y, k, ny), c)) for k in far_first(ny)]
            yield
            for copy in reversed(got):
                copy.wait_recv()

            def use_block(b):
                v = loaded(ab.at[rd, b]).astype(BF16)
                fb[rd, b, here] = v
                use(b, v)

            yield from spread_blocks(lambda b: ab.at[rd, b], use_block)

        acc = [jnp.zeros((n, w1.shape[0]), F32)]

        def use_rows(b):
            acc[0] = acc[0] + dot(rb[b, here], w1[:, cols(b)], (1, 1))

        rb[bid, here] = mine[here, :BLK].astype(BF16)
        cbc[first:first + n_tiles] = jnp.broadcast_to(comb_b, (n, 128)).reshape(n_tiles, SUB, 128)
        for i, p in enumerate(tiled(mine[here])):
            rpart[i, first:first + n_tiles] = p
        yield from spread_blocks(lambda b: rb.at[b, here], use_rows)
        pre = acc[0]
        sigm = jax.nn.sigmoid(pre)
        slope = sigm * (1.0 + pre * (1.0 - sigm))
        bend = sigm * (1.0 - sigm) * (2.0 + pre * (1.0 - 2.0 * sigm))
        hidden = (pre * sigm).astype(BF16)
        hid[0, here] = hidden
        r_piece = rpart[h, pl.ds(first + q * per_q, per_q)]
        c_piece = cbc[pl.ds(first + q * per_q, per_q)]

        mixed = yield from reduce_round(0, lambda b: comb_b * dot(hidden, w2[:, cols(b)], (1, 0)))
        tangent = jnp.tanh(r_piece + mixed)
        sech = 1.0 - tangent * tangent
        upstream = head * sech
        acc[0] = jnp.zeros_like(pre)

        def use_out(b, v):
            acc[0] = acc[0] + dot(v, w2[:, cols(b)], (1, 1))

        yield from gather_round(0, upstream.astype(BF16), use_out)
        back_hidden = comb_b * acc[0]
        back_pre = (back_hidden * slope).astype(BF16)
        hid[1, here] = back_pre

        grad = yield from reduce_round(1, lambda b: dot(back_pre, w1[:, cols(b)], (1, 0)))
        grad = (upstream + grad).astype(BF16)
        acc[0] = jnp.zeros_like(pre)

        def use_in(b, v):
            acc[0] = acc[0] + dot(v, w1[:, cols(b)], (1, 1))

        yield from gather_round(1, grad, use_in)
        second = acc[0]
        push = (comb_b * second * slope).astype(BF16)
        hid[2, here] = push
        ready[first] = True

        pushed = yield from reduce_round(2, lambda b: dot(push, w2[:, cols(b)], (1, 0)))
        curve = (grad.astype(F32) + pushed) * head * (-2.0 * tangent * sech)
        echo = (c_piece * curve).astype(BF16)
        acc[0] = jnp.zeros_like(pre)
        yield from gather_round(2, echo, use_out)
        hid[3, here] = (acc[0] * slope + second * back_hidden * bend).astype(BF16)

    base_tok = slots(nz)
    got_tok = []

    def fill():
        while len(ready) < len(batches):
            yield
        for copy in got_meta:
            copy.wait_recv()
        place = mr[...].astype(F32).reshape(nz * TAIL, META)[:, 0:1]
        home = lax.broadcasted_iota(jnp.int32, (nz * TAIL, 1), 0) // TAIL
        local = place - (z * cap).astype(F32)
        target = jnp.where((local >= 0.0) & (local < cap), local + (home * cap).astype(F32), -1.0)
        pick = lax.broadcasted_iota(jnp.int32, (nz * TAIL, rows), 1).astype(F32)
        pick = jnp.where(pick == target, 1.0, 0.0).astype(BF16)
        for b in range(nb):
            v = dot(pick, fb[1, b], (1, 0))
            ts[:, :, b * BLK:(b + 1) * BLK] = v.reshape(nz, TAIL, BLK).astype(BF16)
        for k in far_first(nz):
            pz = ring(z, k, nz)
            got_tok.append((k, send(ts.at[pz], tr.at[k], base_tok + k, {"dp": pz})))
        yield
        for b in range(nb):
            here = slice(b * BLK, (b + 1) * BLK)
            gi[:, here] = dot(hid[1], fb[1, b], (0, 0))
            go[:, here] = dot(hid[2], fb[0, b], (0, 0))
            if b % 2:
                yield

    drive([chain(i) for i in range(len(batches))] + [fill()])
    for b in range(nb):
        here = slice(b * BLK, (b + 1) * BLK)
        gin_ref[:, here] = (gi[:, here] + dot(hid[3], rb[b], (0, 0))).astype(BF16)
        gout_ref[:, here] = (go[:, here] + dot(hid[0], fb[2, b], (0, 0))).astype(BF16)
    home = ts[z].astype(F32)
    for k, copy in got_tok:
        copy.wait_recv()
        home = home + tr[k].astype(F32)
    r2_ref[...] = home
    for copy in sends:
        copy.wait_send()


def shards(nx, tokens, combine, routes, capacity_slot, readout, weight_in, weight_out, cap=None):
    nz = lax.axis_size("dp")
    ne = lax.axis_size("expert")
    ny = ne // (2 * nx)
    nb = 2 * nx
    pair, d = tokens.shape
    f = weight_in.shape[2]
    if cap is None:
        cap = 5 * pair * ne // (4 * nz)
    rows = nz * cap
    tiles = rows // SUB
    capp = -(-cap // SUB) * SUB
    batches = split_rows(tiles, ny // 2)
    width = BLK + META
    head = readout.reshape(2 * nb, 1, 128)
    vm = pltpu.VMEM
    n_sem = nb + 3 * nz + ny + len(batches) * (2 * nx + 3 * (4 * nx + 2 * ny))
    scratch = [
        vm((f, d), BF16), vm((f, d), BF16), pltpu.SemaphoreType.DMA((2,)),
        pltpu.SemaphoreType.DMA((n_sem,)), pltpu.SemaphoreType.DMA((n_sem,)),
        vm((nb, nb * pair, width), BF16), vm((ny, nb * pair, width), BF16),
        vm((nz, capp // SUB, SUB, width), BF16), vm((nz, capp // SUB, SUB, width), BF16),
        vm((nz, TAIL, META), BF16),
        vm((nb, rows, BLK), BF16), vm((2, tiles, SUB, 128), F32), vm((tiles, SUB, 128), F32),
        vm((3, nb, rows, BLK), BF16), vm((4, rows, f), BF16),
        vm((nz, TAIL, d), BF16), vm((nz, TAIL, d), BF16), vm((f, d), F32), vm((f, d), F32),
        vm((nb, nb * pair, width), BF16), vm((TAIL, META), BF16),
    ]
    for n in batches:
        scratch += [vm((3, nx, 2, n, SUB, 128), BF16)] * 4
        scratch += [vm((3, 2, n, SUB, 128), BF16), vm((3, ny, 2 * n // ny, SUB, 128), BF16)]
        scratch += [vm((3, nb, 2, n, SUB, 128), BF16), vm((2, n, SUB, 128), F32)]
    whole = pl.BlockSpec(memory_space=pltpu.VMEM)
    away = pl.BlockSpec(memory_space=pl.ANY)
    scalars = pl.BlockSpec(memory_space=pltpu.SMEM)
    grad_in, grad_out, home = pl.pallas_call(
        functools.partial(kernel, (nz, nx, ny, cap, batches)),
        out_shape=(
            jax.ShapeDtypeStruct((f, d), BF16), jax.ShapeDtypeStruct((f, d), BF16),
            jax.ShapeDtypeStruct((TAIL, d), F32)),
        in_specs=[scalars, scalars, whole, whole, whole, away, away],
        out_specs=(whole, whole, whole),
        scratch_shapes=scratch,
        compiler_params=pltpu.CompilerParams(
            collective_id=0, has_side_effects=True, vmem_limit_bytes=60000 * 1024),
    )(routes, capacity_slot, combine.reshape(1, pair), tokens, head, weight_in[0].T, weight_out[0])
    steps = 2
    part = d // steps

    def slab(n):
        return pl.BlockSpec((n, part), lambda i: (0, i))

    grad_in, grad_out, r2_grad = pl.pallas_call(
        finish,
        grid=(steps,),
        out_shape=(
            jax.ShapeDtypeStruct((f, d), BF16), jax.ShapeDtypeStruct((f, d), BF16),
            jax.ShapeDtypeStruct((pair, d), BF16)),
        in_specs=[scalars, slab(f), slab(f), slab(TAIL), slab(pair), slab(1)],
        out_specs=(slab(f), slab(f), slab(pair)),
    )(capacity_slot, grad_in, grad_out, home, tokens, readout.reshape(1, d))
    return (r2_grad, grad_in.T[None], grad_out[None])


def solution(mesh, nx=4, cap=None):
    placed = (
        P(("dp", "expert"), None),
        P(("dp", "expert")),
        P(("dp", "expert")),
        P(("dp", "expert")),
        P(),
        P("dp", None, "expert"),
        P("dp", "expert", None),
    )
    return jax.shard_map(
        functools.partial(shards, nx, cap=cap),
        mesh=mesh,
        in_specs=placed,
        out_specs=(P(("dp", "expert"), None), P("dp", None, "expert"), P("dp", "expert", None)),
        check_vma=False,
    )
```
